512 devices in a mesh: tok: 64 (over y, z), head: 8 (over x, core).
Axes of the slice: x: 4, y: 4, z: 16, core: 2. Of those that a mesh axis runs over, the one named last changes fastest.
Arguments:
- hidden: bfloat16 [106496, 5120], P('tok', 'head'), may hold values from -6 to 6
- w_latent: bfloat16 [5120, 512], P('head'), may hold values from -0.078125 to 0.078125
- w_rope: bfloat16 [5120, 64], P('head'), may hold values from -0.078125 to 0.078125
- kv_gain: float32 [512], replicated, may hold values from 0.25 to 1.75
- q_latent: bfloat16 [64, 32, 64, 512], P('tok', None, 'head'), may hold values from -105 to 105
- q_rope: bfloat16 [64, 32, 4096], P('tok', None, 'head'), may hold values from -6 to 6
- w_value: bfloat16 [64, 512, 128], P('head'), may hold values from -0.25 to 0.25
- page_table: int32 [64, 32], replicated, may hold values from -1 to 831, as said below
- dest_group: int32 [64], replicated, may hold values from 0 to 63, each once
- ctx_len: int32 [64], replicated, may hold values from 1 to 4096, as said below
Outputs:
- attn_out: bfloat16 [64, 32, 8192], P('tok', 'head')
The draws below stay inside these ranges and needn't reach their ends.
Inputs may be any that keep to these rules, and one draw needn't show every extreme that they name: `page_table`: row r lists request r's pages in context order, then -1; every page appears in exactly one row; no row holds two pages p whose p // 13 is equal; some row holds 32 pages. Request r's listed pages number ctx_len[r] / 128 rounded up. `dest_group`: every group serves exactly one request.
All inputs are finite; a program needn't handle non-finite values.
Results may differ from the reference program's by a relative error of at most 0.012.
The reference program's roundings to bfloat16 on the way count: a program that leaves them out, or rounds other values in their place, can miss the bound.
Values may be sent and summed in bfloat16 or wider, within the bound.
A program may use at most 64 MiB of HBM per device.

```python
import jax
import jax.numpy as jnp
from jax import lax

D = 5120
LAT = 512
ROPE = 64
VDIM = 128
H = 64
PAGE = 128
ROWS = 32
BLOCK = 4
PAGES_DEV = 13
GROUPS = 64
TOKENS = 106496
NPAGES = 832
MAXP = 32
MAXPAD = 32


def page_plan(key):
    base_key = jax.random.fold_in(key, 7)
    chosen_key, weight_key, source_key, within_key = jax.random.split(base_key, 4)
    page_count = GROUPS * PAGES_DEV
    chosen = jax.random.randint(chosen_key, (), 0, GROUPS)
    weights = jax.random.randint(weight_key, (GROUPS,), 1, 9)
    request_ids = jnp.arange(GROUPS, dtype=jnp.int32)
    counts = jnp.where(request_ids == chosen, MAXP, 1).astype(jnp.int32)
    surplus = page_count - MAXP - (GROUPS - 1)
    big_score = 1 << 30

    def add_unit(unit_step, counts_now):
        eligible = (request_ids != chosen) & (counts_now < MAXP)
        ranking = jnp.where(eligible, counts_now * 840 // weights * GROUPS + request_ids, big_score)
        winner = jnp.argmin(ranking)
        return counts_now + (request_ids == winner).astype(jnp.int32)
    counts = lax.fori_loop(0, surplus, add_unit, counts)
    source_order = jax.random.permutation(source_key, GROUPS).astype(jnp.int32)
    within_order = jax.vmap(lambda subkey: jax.random.permutation(subkey, PAGES_DEV))(jax.random.split(within_key, GROUPS)).astype(jnp.int32)
    starts = jnp.cumsum(counts) - counts
    column_ids = jnp.arange(MAXP, dtype=jnp.int32)
    entry = jnp.minimum(starts[:, None] + column_ids[None, :], page_count - 1)
    source = source_order[entry % GROUPS]
    local_slot = within_order[source, entry // GROUPS]
    page_rows = jnp.where(column_ids[None, :] < counts[:, None], source * PAGES_DEV + local_slot, -1)
    return (page_rows.astype(jnp.int32), counts)


def draw_page_table(key, part):
    return page_plan(key)[0]


def draw_ctx_len(key, part):
    counts = page_plan(key)[1]
    trimmed = jax.random.randint(jax.random.fold_in(key, 11), (GROUPS,), 0, PAGE)
    return (counts * PAGE - trimmed).astype(jnp.int32)


def draw_q_latent(key, part):
    first_key = jax.random.fold_in(jax.random.fold_in(key, 3), 0)
    full_shape = (GROUPS, ROWS, H, LAT)
    values_drawn = jnp.clip(jax.random.normal(first_key, full_shape, jnp.float32) * 1.5, -9.0, 9.0)
    return values_drawn.astype(jnp.bfloat16)


def steps_of(own_key, dims, cuts, least, high):
    level, own = 1.0, jax.random.fold_in(own_key, 6)
    for axis_at, parts in cuts:
        draws = jnp.exp(jax.random.uniform(jax.random.fold_in(own, axis_at), (parts,), jnp.float32, least / len(cuts), high / len(cuts)))
        level = level * jnp.repeat(draws, dims[axis_at] // parts).reshape([-1 if axis == axis_at else 1 for axis in range(len(dims))])
    return level


def noise(rng, shape, width, bound, pieces=(), kind=jnp.bfloat16):
    array = jax.random.normal(rng, shape, jnp.float32) * width
    if len(pieces) > 0:
        array = steps_of(rng, shape, pieces, -0.22, 0.18) * array
    return jnp.clip(array, min=-bound, max=bound).astype(kind)


def setup_inputs(seed: int = 0) -> dict:
    splits = jax.random.split(jax.random.key(seed), 11)
    hidden = noise(splits[0], (TOKENS, D), 1.0, 6.0, ((0, 64), (1, 8)))
    w_latent = noise(splits[1], (D, LAT), D ** -0.5, 0.078125, ((0, 8),))
    w_rope = noise(splits[2], (D, ROPE), D ** -0.5, 0.078125, ((0, 8),))
    kv_gain = jnp.clip(1.0 + 0.15 * jax.random.normal(splits[3], (LAT,), jnp.float32), 0.25, 1.75)
    q_latent = draw_q_latent(jax.random.fold_in(splits[10], 71), 0)
    q_rope = noise(splits[5], (GROUPS, ROWS, H * ROPE), 1.0, 6.0, ((0, 64), (2, 8)))
    w_value = noise(splits[6], (H, LAT, VDIM), LAT ** -0.5, 0.25, ((0, 8),))
    page_table = draw_page_table(jax.random.fold_in(splits[10], 71), 0)
    dest_group = jax.random.permutation(splits[8], GROUPS).astype(jnp.int32)
    ctx_len = draw_ctx_len(jax.random.fold_in(splits[10], 71), 0)
    return dict(hidden=hidden, w_latent=w_latent, w_rope=w_rope, kv_gain=kv_gain, q_latent=q_latent, q_rope=q_rope, w_value=w_value, page_table=page_table, dest_group=dest_group, ctx_len=ctx_len)


EPS = 1e-06
SCALE = 192.0 ** (-0.5)
THETA = 10000.0
FLOOR = -1e+30

def normalize(latent_sum, kv_gain):
    inverse = lax.rsqrt(lax.optimization_barrier(jnp.mean(latent_sum * latent_sum, axis=-1, keepdims=True)) + EPS)
    return (latent_sum * inverse * kv_gain).astype(jnp.bfloat16)

def rotate_keys(raw_rope):
    page_total, rope_width, page_len = raw_rope.shape
    half_width = rope_width // 2
    frequency = THETA ** (-2.0 * jnp.arange(half_width, dtype=jnp.float32) / rope_width)
    positions = (jnp.arange(page_total, dtype=jnp.int32)[:, None] * page_len + jnp.arange(page_len, dtype=jnp.int32)[None, :]).astype(jnp.float32)
    angles = frequency[None, :, None] * positions[:, None, :]
    cosine = jnp.cos(angles)
    sine_part = jnp.sin(angles)
    values = raw_rope.astype(jnp.float32)
    first_half = values[:, :half_width]
    second = values[:, half_width:]
    rotated = jnp.concatenate([first_half * cosine - second * sine_part, second * cosine + first_half * sine_part], axis=1)
    return rotated.astype(jnp.bfloat16)

def attend(query_latent, query_rope, key_pages, rope_pages, context):
    page_total, page_len, lat_width = key_pages.shape
    flat_keys = key_pages.reshape(page_total * page_len, lat_width).astype(jnp.float32)
    rope_keys = rope_pages.astype(jnp.float32)
    query_main = query_latent.astype(jnp.float32)
    query_side = query_rope.astype(jnp.float32)
    row_count, head_count = (query_latent.shape[0], query_latent.shape[1])
    block_rows = BLOCK * page_len
    blocks_used = (context + block_rows - 1) // block_rows

    def block_step(block_index, state_now):
        running_max, denominator, accumulated = state_now
        key_block = lax.dynamic_slice_in_dim(flat_keys, block_index * block_rows, block_rows, 0)
        rope_block = lax.dynamic_slice_in_dim(rope_keys, block_index * BLOCK, BLOCK, 0)
        scores = jnp.einsum('rhl,kl->rhk', query_main, key_block)
        scores = scores + jnp.einsum('rhe,jek->rhjk', query_side, rope_block).reshape(row_count, head_count, block_rows)
        scores = scores * SCALE
        positions = block_index * block_rows + jnp.arange(block_rows, dtype=jnp.int32)
        scores = jnp.where(positions < context, scores, FLOOR)
        new_max = jnp.maximum(running_max, lax.optimization_barrier(jnp.max(scores, axis=-1)))
        factor = jnp.exp(running_max - new_max)
        probabilities = jnp.exp(scores - new_max[..., None])
        denominator = denominator * factor + lax.optimization_barrier(jnp.sum(probabilities, axis=-1))
        rounded = lax.optimization_barrier(probabilities.astype(jnp.bfloat16)).astype(jnp.float32)
        accumulated = accumulated * factor[..., None] + jnp.einsum('rhk,kl->rhl', rounded, key_block)
        return (new_max, denominator, accumulated)
    start_state = (jnp.full((row_count, head_count), FLOOR, jnp.float32), jnp.zeros((row_count, head_count), jnp.float32), jnp.zeros((row_count, head_count, lat_width), jnp.float32))
    running_max, denominator, accumulated = lax.fori_loop(0, blocks_used, block_step, start_state)
    return (accumulated / denominator[..., None]).astype(jnp.bfloat16)

def reference(hidden, w_latent, w_rope, kv_gain, q_latent, q_rope, w_value, page_table, dest_group, ctx_len):
    latent_sum = jnp.dot(hidden, w_latent, preferred_element_type=jnp.float32)
    latent_cache = lax.optimization_barrier(normalize(latent_sum, kv_gain)).reshape(NPAGES, PAGE, LAT)
    raw_rope = lax.optimization_barrier(jnp.dot(hidden, w_rope, preferred_element_type=jnp.float32).astype(jnp.bfloat16))
    raw_rope = raw_rope.reshape(NPAGES, PAGE, ROPE).transpose(0, 2, 1)
    filler = -jnp.ones((GROUPS, MAXPAD - MAXP), jnp.int32)
    page_rows = jnp.concatenate([page_table.astype(jnp.int32), filler], axis=1)
    value_maps = w_value.astype(jnp.float32)

    def serve_group(group_id):
        served_here = dest_group == group_id
        page_list = lax.optimization_barrier(jnp.sum(jnp.where(served_here[:, None], page_rows, 0), axis=0)).astype(jnp.int32)
        context = jnp.sum(jnp.where(served_here, ctx_len, 0)).astype(jnp.int32)
        safe_list = jnp.clip(page_list, 0, NPAGES - 1)
        key_pages = latent_cache[safe_list]
        rope_pages = rotate_keys(raw_rope[safe_list])
        query_side = q_rope[group_id].reshape(ROWS, H, ROPE)
        attended = attend(q_latent[group_id], query_side, key_pages, rope_pages, context)
        attended = lax.optimization_barrier(attended).astype(jnp.float32)
        mapped = jnp.einsum('rhl,hlv->rhv', attended, value_maps)
        return mapped.astype(jnp.bfloat16).reshape(ROWS, H * VDIM)
    return lax.map(serve_group, jnp.arange(GROUPS, dtype=jnp.int32))
```

```python
import functools

import jax
import jax.numpy as jnp
from jax import lax
from jax.experimental import pallas as pl
from jax.experimental.pallas import tpu as pltpu
from jax.sharding import PartitionSpec as P

PAGE = 128
BLOCK = 4
EPS = 1e-06
SCALE = 192.0 ** (-0.5)
THETA = 10000.0
FLOOR = -1e30
MESH = pl.DeviceIdType.MESH
LAT = 512
WIDE = 640
VMEM_BYTES = 60 * 1024 * 1024


def cut_along(value, dim, size):
    dims = value.shape
    pieces = value.reshape(*dims[:dim], size, dims[dim] // size, *dims[dim + 1 :])
    return jnp.moveaxis(pieces, dim, 0)


def summed_on_arrival(value, axis, dim):
    pieces = cut_along(value, dim, lax.axis_size(axis))
    arrived = lax.all_to_all(pieces, axis, split_axis=0, concat_axis=0, tiled=True)
    return arrived.sum(axis=0)


def sent_together(arrays, axis, split_dim, concat_dim, along):
    columns = [a.reshape(*a.shape[:along], -1) for a in arrays]
    both = jnp.concatenate(columns, axis=along)
    whole, at, done = (
        lax.all_to_all(both, axis, split_axis=split_dim, concat_axis=concat_dim, tiled=True),
        0,
        [],
    )
    for a, column in zip(arrays, columns):
        piece = whole[..., at : at + column.shape[along]]
        done.append(piece.reshape(*piece.shape[:along], *a.shape[along:]))
        at += column.shape[along]
    return tuple(done)


def normalize(latent_sum, kv_gain):
    inverse = lax.rsqrt(jnp.mean(latent_sum * latent_sum, axis=-1, keepdims=True) + EPS)
    return (latent_sum * inverse * kv_gain).astype(jnp.bfloat16)


def rotate_rows(raw, positions):
    width = raw.shape[-1]
    half = width // 2
    frequency = THETA ** (-2.0 * jnp.arange(half, dtype=jnp.float32) / width)
    angles = positions.astype(jnp.float32)[:, None] * frequency[None, :]
    cosine, sine = jnp.cos(angles), jnp.sin(angles)
    values = raw.astype(jnp.float32)
    first, second = values[:, :half], values[:, half:]
    turned = [first * cosine - second * sine, second * cosine + first * sine]
    return jnp.concatenate(turned, axis=1).astype(jnp.bfloat16)


def greet(peers):
    barrier = pltpu.get_barrier_semaphore()
    for peer in peers:
        pl.semaphore_signal(barrier, inc=1, device_id=peer, device_id_type=MESH)
    pl.semaphore_wait(barrier, len(peers))


def attend_kernel(
    place, ctx_ref, q_ref, share_ref, wv_ref, out_ref,
    kbuf, top, total, acc, att, put, got, send_sem, recv_sem, out_send, out_recv,
):
    me = lax.axis_index("head")
    core = lax.rem(me, 2)
    x = lax.div(me, 2)
    other = me + 1 - 2 * core

    def at(dx, c):
        return lax.rem(x + dx, 4) * 2 + c

    greet([{"head": lax.rem(me + k, 8)} for k in range(1, 8)])
    keys = share_ref.shape[0]
    half = keys // 2

    def send(number, src, dst, to):
        copy = pltpu.make_async_remote_copy(
            src_ref=src, dst_ref=dst, send_sem=send_sem.at[number],
            recv_sem=recv_sem.at[number], device_id={"head": to}, device_id_type=MESH,
        )
        copy.start()
        return copy

    left, right, across = at(3, core), at(1, core), at(2, core)
    to_right = send(0, share_ref, kbuf.at[me], right)
    to_left = send(1, share_ref, kbuf.at[me], left)
    to_other = send(2, share_ref, kbuf.at[me], other)
    ctx = ctx_ref[0]
    top[...] = jnp.full_like(top, FLOOR)
    total[...] = jnp.zeros_like(total)
    acc[...] = jnp.zeros_like(acc)

    def process(block, owner):
        lane = lax.broadcasted_iota(jnp.int32, (1, keys), 1)
        live = place(lane, owner) < ctx

        def step(i, _):
            rows = pl.ds(pl.multiple_of(i * 128, 128), 128)
            scores = lax.dot_general(
                q_ref[rows, :], block[...], (((1,), (1,)), ((), ())),
                preferred_element_type=jnp.float32,
            )
            scores = jnp.where(live, scores * SCALE, FLOOR)
            old = top[rows, :]
            new = jnp.maximum(old, jnp.max(scores, axis=-1, keepdims=True))
            factor = jnp.exp(old - new)
            probs = jnp.exp(scores - new)
            top[rows, :] = new
            total[rows, :] = total[rows, :] * factor + jnp.sum(probs, axis=-1, keepdims=True)
            acc[rows, :] = acc[rows, :] * factor + jnp.dot(
                probs.astype(jnp.bfloat16), block[:, :LAT], preferred_element_type=jnp.float32
            )
            return 0

        lax.fori_loop(0, q_ref.shape[0] // 128, step, 0)

    process(share_ref, me)
    to_other.wait_recv()
    process(kbuf.at[other], other)
    to_right.wait_recv()
    on_right = send(3, kbuf.at[left, pl.ds(0, half)], kbuf.at[left, pl.ds(0, half)], right)
    to_left.wait_recv()
    on_left = send(4, kbuf.at[right, pl.ds(half, half)], kbuf.at[right, pl.ds(half, half)], left)
    pass_left = send(5, kbuf.at[left], kbuf.at[left], other)
    pass_right = send(6, kbuf.at[right], kbuf.at[right], other)
    process(kbuf.at[left], left)
    process(kbuf.at[right], right)
    pass_left.wait_recv()
    process(kbuf.at[at(3, 1 - core)], at(3, 1 - core))
    pass_right.wait_recv()
    process(kbuf.at[at(1, 1 - core)], at(1, 1 - core))
    on_right.wait_recv()
    on_left.wait_recv()
    pass_across = send(7, kbuf.at[across], kbuf.at[across], other)
    process(kbuf.at[across], across)
    pass_across.wait_recv()
    process(kbuf.at[at(2, 1 - core)], at(2, 1 - core))
    for copy in (to_right, to_left, to_other, on_right, on_left, pass_left, pass_right, pass_across):
        copy.wait_send()

    att[...] = (acc[...] / total[...]).astype(jnp.bfloat16)
    rows = att.shape[0] // 8
    for h in range(8):
        mapped = jnp.dot(
            att[h * rows : (h + 1) * rows, :], wv_ref[h], preferred_element_type=jnp.float32
        )
        for d in range(8):
            put[d, :, h * 128 : (h + 1) * 128] = mapped[4 * d : 4 * d + 4]
    copies = []
    for k in range(1, 8):
        to = lax.rem(me + k, 8)
        copy = pltpu.make_async_remote_copy(
            src_ref=put.at[to], dst_ref=got.at[me], send_sem=out_send.at[k],
            recv_sem=out_recv.at[k], device_id={"head": to}, device_id_type=MESH,
        )
        copy.start()
        copies.append(copy)
    got[me] = put[me]
    for copy in copies:
        copy.wait()
    for s in range(8):
        out_ref[:, s * 1024 : (s + 1) * 1024] = got[s].astype(jnp.bfloat16)


def gather_and_attend(place, context, queries, share, w_value):
    keys = share.shape[0]
    count = queries.shape[0]
    vmem = pl.BlockSpec(memory_space=pltpu.VMEM)
    return pl.pallas_call(
        functools.partial(attend_kernel, place),
        out_shape=jax.ShapeDtypeStruct((4, 8192), jnp.bfloat16),
        in_specs=[pl.BlockSpec(memory_space=pltpu.SMEM), vmem, vmem, vmem],
        out_specs=vmem,
        scratch_shapes=[
            pltpu.VMEM((8, keys, WIDE), jnp.bfloat16),
            pltpu.VMEM((count, 1), jnp.float32),
            pltpu.VMEM((count, 1), jnp.float32),
            pltpu.VMEM((count, LAT), jnp.float32),
            pltpu.VMEM((count, LAT), jnp.bfloat16),
            pltpu.VMEM((8, 4, 1024), jnp.float32),
            pltpu.VMEM((8, 4, 1024), jnp.float32),
            pltpu.SemaphoreType.DMA((8,)),
            pltpu.SemaphoreType.DMA((8,)),
            pltpu.SemaphoreType.DMA((8,)),
            pltpu.SemaphoreType.DMA((8,)),
        ],
        compiler_params=pltpu.CompilerParams(
            collective_id=2, has_side_effects=True, vmem_limit_bytes=VMEM_BYTES
        ),
        name="gather_attend",
    )(context.reshape(1), queries, share, w_value)


def place_rows(lane, owner):
    return lax.shift_right_logical(lane, 4) * PAGE + owner * 16 + lax.bitwise_and(lane, 15)


def pack_queries(q_latent, q_rope):
    rows, heads = q_latent.shape[1], q_latent.shape[2]
    side = q_rope[0].reshape(rows, heads, -1)
    both = jnp.concatenate(
        [q_latent[0], side, jnp.zeros((rows, heads, WIDE - LAT - side.shape[-1]), jnp.bfloat16)], -1
    )
    return jnp.swapaxes(both, 0, 1).reshape(rows * heads, WIDE)


def per_device(
    hidden, w_latent, w_rope, kv_gain, q_latent, q_rope, w_value, page_table, dest_group, ctx_len
):
    groups = lax.axis_size("tok")
    my_index = lax.axis_index("tok")
    pages_here = hidden.shape[0] // PAGE
    slices = hidden.reshape(pages_here, PAGE, hidden.shape[1])
    latent_terms = jnp.einsum("pkd,dl->pkl", slices, w_latent, preferred_element_type=jnp.float32)
    rope_terms = jnp.einsum("pkd,de->pek", slices, w_rope, preferred_element_type=jnp.float32)
    page_ids = my_index * pages_here + jnp.arange(pages_here, dtype=jnp.int32)
    claimed = jnp.any(page_table[:, :, None] == page_ids[None, None, :], axis=1)
    group_ids = jnp.arange(groups, dtype=jnp.int32)
    served = dest_group[:, None] == group_ids[None, :]
    routing = jnp.dot(
        served.astype(jnp.bfloat16).T,
        claimed.astype(jnp.bfloat16),
        preferred_element_type=jnp.float32,
    ).astype(jnp.bfloat16)
    served_here = dest_group == my_index
    page_list = jnp.sum(jnp.where(served_here[:, None], page_table, 0), axis=0)
    context = jnp.sum(jnp.where(served_here, ctx_len, 0))
    list_len = page_table.shape[1]
    padded_len = (list_len + BLOCK - 1) // BLOCK * BLOCK
    sources = jnp.concatenate(
        [page_list // pages_here, -jnp.ones((padded_len - list_len,), jnp.int32)]
    )
    select = (sources[:, None] == group_ids[None, :]).astype(jnp.bfloat16)
    latent_share, rope_share = (
        summed_on_arrival(latent_terms, "head", 1),
        summed_on_arrival(rope_terms, "head", 2),
    )
    send_latent = jnp.einsum(
        "gp,pkl->gkl", routing, normalize(latent_share, kv_gain), preferred_element_type=jnp.float32
    ).astype(jnp.bfloat16)
    send_rope = jnp.einsum(
        "gp,pek->gek", routing, rope_share.astype(jnp.bfloat16), preferred_element_type=jnp.float32
    ).astype(jnp.bfloat16)
    send_latent, send_rope = (send_latent, send_rope)
    arrived_latent, arrived_rope = sent_together((send_latent, send_rope), "tok", 0, 0, 1)
    picked_latent = jnp.einsum(
        "jg,gkl->jkl", select, arrived_latent, preferred_element_type=jnp.float32
    ).astype(jnp.bfloat16)
    picked_rope = jnp.einsum(
        "jg,gek->jek", select, arrived_rope, preferred_element_type=jnp.float32
    ).astype(jnp.bfloat16)
    owner = lax.axis_index("head")
    count = padded_len * 16
    positions = place_rows(jnp.arange(count, dtype=jnp.int32), owner)
    rotated = rotate_rows(jnp.swapaxes(picked_rope, 1, 2).reshape(count, -1), positions)
    share = jnp.concatenate(
        [
            picked_latent.reshape(count, LAT),
            rotated,
            jnp.zeros((count, WIDE - LAT - rotated.shape[-1]), jnp.bfloat16),
        ],
        axis=1,
    )
    queries = pack_queries(q_latent, q_rope)
    return gather_and_attend(place_rows, context, queries, share, w_value)[None]


def solution(mesh):
    placed = (
        P("tok", "head"),
        P("head", None),
        P("head", None),
        P(),
        P("tok", None, "head", None),
        P("tok", None, "head"),
        P("head", None, None),
        P(),
        P(),
        P(),
    )
    return jax.shard_map(
        per_device, mesh=mesh, in_specs=placed, out_specs=P("tok", "head", None), check_vma=False
    )
```
